32 devices in a mesh: group: 4 (over y, core), member: 8 (over z, x).
Axes of the slice: x: 2, y: 2, z: 4, core: 2. Of those that a mesh axis runs over, the one named last changes fastest.
Arguments:
- tokens: bfloat16 [128, 196, 768], P(('group', 'member')), may hold values from -6 to 6
- w_query: bfloat16 [768, 768], replicated, may hold values from -8 to 8
- w_key: bfloat16 [768, 768], replicated, may hold values from -1 to 1
- w_value: bfloat16 [768, 768], replicated, may hold values from -0.21875 to 0.21875
- w_out: bfloat16 [768, 768], replicated, may hold values from -0.21875 to 0.21875
- partners: int32 [128, 4], P(('group', 'member')), may hold values from 0 to 127, as said below
- counts: int32 [128], P(('group', 'member')), may hold values from 1 to 4
- key_slot: int32 [32], P(('group', 'member')), may hold values from 0 to 3
Outputs:
- refined: bfloat16 [128, 196, 768], P(('group', 'member'))
The draws below stay inside these ranges and needn't reach their ends.
Inputs may be any that keep to these rules, and one draw needn't show every extreme that they name: `partners`: every entry names a view held by another device of the same group; the entries of all views of one device name views of one other device at most 3 times, and those of some other device exactly 3 times.
All inputs are finite; a program needn't handle non-finite values.
Results may differ from the reference program's by a relative error of at most 0.011.
Values may be sent and summed in bfloat16 or wider, within the bound.
A program may use at most 128 MiB of HBM per device.

```python
import jax
import jax.numpy as jnp
from jax import lax

D = 768
HEADS = 12
SEQ = 196
DEG = 4
VIEWS_DEV = 4
VIEWS = 128
N_GROUP = 4
N_MEMBER = 8


def draw_tokens(key, part):
    normal_draw = jax.random.normal(key, (VIEWS, SEQ, D), jnp.float32)
    return jnp.clip(normal_draw, -6.0, 6.0).astype(jnp.bfloat16)


def weight_pair(key):
    pair_key = jax.random.fold_in(key, 101)
    key_matrix = jax.random.normal(jax.random.fold_in(pair_key, 1), (D, D), jnp.float32) / jnp.sqrt(jnp.float32(D))
    query_matrix = jax.random.normal(jax.random.fold_in(pair_key, 2), (D, D), jnp.float32) / jnp.sqrt(jnp.float32(D))
    return (jnp.clip(query_matrix, -8.0, 8.0), jnp.clip(key_matrix, -1.0, 1.0))


def draw_w_query(key, part):
    return weight_pair(key)[0].astype(jnp.bfloat16)


def draw_w_key(key, part):
    return weight_pair(key)[1].astype(jnp.bfloat16)


def draw_partners(key, part):
    devices_all = N_GROUP * N_MEMBER
    entry_count = VIEWS_DEV * DEG
    rotation = jax.random.randint(jax.random.fold_in(key, 11), (devices_all, 1), 0, N_MEMBER - 1)
    slots = jax.random.randint(jax.random.fold_in(key, 12), (devices_all, entry_count), 0, VIEWS_DEV)
    device_ids = jnp.arange(devices_all, dtype=jnp.int32)[:, None]
    entry_ids = jnp.arange(entry_count, dtype=jnp.int32)[None, :]
    group_index = device_ids // N_MEMBER
    member_index = device_ids % N_MEMBER
    peers = (member_index + 1 + (entry_ids + rotation) % (N_MEMBER - 1)) % N_MEMBER
    views = (group_index * N_MEMBER + peers) * VIEWS_DEV + slots
    return views.reshape(VIEWS, DEG).astype(jnp.int32)


def with_ends(values, key, low, top_value):
    dims = values.shape
    place = [jax.random.randint(jax.random.fold_in(key, axis), (), 0, dims[axis]) for axis in range(len(dims))]
    values = values.at[tuple(place)].set(low)
    longest = dims.index(max(dims))
    place[longest] = (place[longest] + 1) % dims[longest]
    return values.at[tuple(place)].set(top_value)


def centred(own_key, extent, width, bound, kind=jnp.bfloat16):
    values = width * jax.random.normal(own_key, extent, jnp.float32)
    return jnp.clip(values, min=-bound, max=bound).astype(kind)


def setup_inputs(seed: int = 0) -> dict:
    seeds = jax.random.split(jax.random.key(seed), 9)
    tokens = draw_tokens(jax.random.fold_in(seeds[8], 71), 0)
    w_query = draw_w_query(jax.random.fold_in(seeds[8], 71), 0)
    w_key = draw_w_key(jax.random.fold_in(seeds[8], 71), 0)
    w_value = centred(seeds[3], (D, D), D ** -0.5, 0.21875)
    w_out = centred(seeds[4], (D, D), D ** -0.5, 0.21875)
    partners = draw_partners(jax.random.fold_in(seeds[8], 71), 0)
    counts = with_ends(jax.random.randint(seeds[6], (VIEWS,), 1, DEG + 1), jax.random.fold_in(seeds[6], 1), 1, DEG).astype(jnp.int32)
    key_slot = with_ends(jax.random.randint(seeds[7], (N_GROUP * N_MEMBER,), 0, VIEWS_DEV), jax.random.fold_in(seeds[7], 1), 0, VIEWS_DEV - 1).astype(jnp.int32)
    return {"tokens": tokens, "w_query": w_query, "w_key": w_key, "w_value": w_value, "w_out": w_out, "partners": partners, "counts": counts, "key_slot": key_slot}


def layer_norm(values_in):
    values_in = values_in.astype(jnp.float32)
    centre = lax.optimization_barrier(jnp.mean(values_in, axis=-1, keepdims=True))
    spread = lax.optimization_barrier(jnp.mean((values_in - centre) ** 2, axis=-1, keepdims=True))
    return (values_in - centre) * lax.rsqrt(spread + 1e-05)

def attend(view_query, key_block, value_block, head_count):
    length, features = view_query.shape
    head_size = features // head_count
    entries = key_block.shape[0]
    query_heads = view_query.astype(jnp.float32).reshape(length, head_count, head_size)
    key_heads = key_block.astype(jnp.float32).reshape(entries, length, head_count, head_size)
    value_heads = value_block.astype(jnp.float32).reshape(entries, length, head_count, head_size)
    scores = jnp.einsum('qhd,ekhd->ehqk', query_heads, key_heads) / jnp.sqrt(jnp.float32(head_size))
    probabilities = jax.nn.softmax(scores, axis=-1).astype(jnp.bfloat16)
    outputs = jnp.einsum('ehqk,ekhd->eqhd', probabilities.astype(jnp.float32), value_heads)
    return outputs.reshape(entries, length, features)

def reference(tokens, w_query, w_key, w_value, w_out, partners, counts, key_slot):
    views, length, features = tokens.shape
    normed = layer_norm(tokens).astype(jnp.bfloat16)
    flat_rows = normed.reshape(views * length, features)
    queries = jnp.dot(flat_rows, w_query, preferred_element_type=jnp.float32).astype(jnp.bfloat16).reshape(views, length, features)
    keys_all = jnp.dot(flat_rows, w_key, preferred_element_type=jnp.float32).astype(jnp.bfloat16).reshape(views, length, features)
    values_all = jnp.dot(flat_rows, w_value, preferred_element_type=jnp.float32).astype(jnp.bfloat16).reshape(views, length, features)

    def one_view(view_id):
        device = view_id // VIEWS_DEV
        group_index = device // N_MEMBER
        member_index = device % N_MEMBER
        keyframe = (view_id % VIEWS_DEV == key_slot[device]).astype(jnp.int32)
        below_dev = (group_index - 1) % N_GROUP * N_MEMBER + member_index
        above_dev = (group_index + 1) % N_GROUP * N_MEMBER + member_index
        below_key = below_dev * VIEWS_DEV + key_slot[below_dev]
        above_key = above_dev * VIEWS_DEV + key_slot[above_dev]
        partner_ids = jnp.concatenate([partners[view_id], jnp.stack([below_key, above_key]).astype(jnp.int32)]).astype(jnp.int32)
        outputs = attend(queries[view_id], keys_all[partner_ids], values_all[partner_ids], HEADS)
        divisor = (counts[view_id] + 2 * keyframe).astype(jnp.float32)
        live_weight = (jnp.arange(DEG, dtype=jnp.int32) < counts[view_id]).astype(jnp.float32)
        key_weight = jnp.full((2,), keyframe, jnp.int32).astype(jnp.float32)
        pair_weights = jnp.concatenate([live_weight, key_weight]) / divisor
        return lax.optimization_barrier(jnp.sum(pair_weights[:, None, None] * outputs, axis=0)).astype(jnp.bfloat16)
    mixed = lax.map(one_view, jnp.arange(views, dtype=jnp.int32))
    projected = jnp.dot(mixed.reshape(views * length, features), w_out, preferred_element_type=jnp.float32)
    refined = tokens.astype(jnp.float32) + projected.reshape(views, length, features)
    return refined.astype(jnp.bfloat16)
```

```python
import functools

import jax
import jax.numpy as jnp
from jax import lax
from jax.experimental import pallas as pl
from jax.experimental.pallas import tpu as pltpu
from jax.sharding import PartitionSpec as P

HEADS = 12
ROW = 2


def layer_norm(values_in):
    values_in = values_in.astype(jnp.float32)
    centre = jnp.mean(values_in, axis=-1, keepdims=True)
    spread = jnp.mean((values_in - centre) ** 2, axis=-1, keepdims=True)
    return (values_in - centre) * lax.rsqrt(spread + 1e-05)


def step_kernel(phase, first, final, places, *refs):
    table, queries, w_pair = refs[:3]
    blocks = refs[3 : 3 + len(places)]
    rest = list(refs[3 + len(places) :])
    if not first:
        total_in = rest.pop(0)
    if final:
        inverse, tokens, w_out = rest[:3]
        rest = rest[3:]
    out_ref = rest.pop(0)
    held, pair, total, sems = rest
    copies = [
        pltpu.make_async_copy(block, held.at[pl.ds(place, block.shape[0])], sems.at[i])
        for i, (place, block) in enumerate(zip(places, blocks))
    ]
    if not first:
        copies.append(pltpu.make_async_copy(total_in, total, sems.at[len(copies)]))
    for copy in copies:
        copy.start()
    if first:
        total[...] = jnp.zeros_like(total)
    for copy in copies:
        copy.wait()
    views, length, features = queries.shape
    size = features // HEADS
    lanes = lax.broadcasted_iota(jnp.int32, (1, 2 * size), 1)
    lower = lanes < size

    def entry(e, carry):
        @pl.when(table[0, e] == phase)
        def _():
            place, view = table[1, e], table[2, e]
            normed = layer_norm(held[place]).astype(jnp.bfloat16)
            pair[...] = jnp.dot(
                normed, w_pair[...], preferred_element_type=jnp.float32
            ).astype(jnp.bfloat16)
            for h in range(HEADS // 2):
                cols = pl.ds(2 * h * size, 2 * size)
                query = queries[view, :, cols] * jnp.bfloat16(size**-0.5)
                key = pair[:, cols]
                value = pair[:, pl.ds(features + 2 * h * size, 2 * size)]
                halves = []
                for keep in (lower, jnp.logical_not(lower)):
                    part = jnp.where(keep, query, jnp.zeros_like(query))
                    scores = lax.dot_general(
                        part, key, (((1,), (1,)), ((), ())), preferred_element_type=jnp.float32
                    )
                    top = jnp.max(scores, axis=-1, keepdims=True)
                    weights = jnp.exp(scores - top)
                    mass = jnp.sum(weights, axis=-1, keepdims=True)
                    result = jnp.dot(
                        weights.astype(jnp.bfloat16), value, preferred_element_type=jnp.float32
                    )
                    halves.append(result / mass)
                total[view, :, cols] += jnp.where(lower, halves[0], halves[1])

        return carry

    lax.fori_loop(0, table.shape[1], entry, 0)
    if final:
        for v in range(views):
            mixed = (total[v] * inverse[v]).astype(jnp.bfloat16)
            projected = jnp.dot(mixed, w_out[...], preferred_element_type=jnp.float32)
            out_ref[v] = (tokens[v].astype(jnp.float32) + projected).astype(out_ref.dtype)
    else:
        copy = pltpu.make_async_copy(total, out_ref, sems.at[0])
        copy.start()
        copy.wait()


def add_phase(phase, table, queries, w_pair, blocks, total, finish=None):
    views, length, features = queries.shape
    first, final = total is None, finish is not None
    places = [place for place, _ in blocks]
    arrays = [block for _, block in blocks]
    depth = max(place + block.shape[0] for place, block in blocks)
    vmem = pl.BlockSpec(memory_space=pltpu.VMEM)
    smem = pl.BlockSpec(memory_space=pltpu.SMEM)
    hbm = pl.BlockSpec(memory_space=pl.ANY)
    operands = [table, queries, w_pair, *arrays]
    specs = [smem, vmem, vmem] + [hbm] * len(arrays)
    if not first:
        operands.append(total)
        specs.append(hbm)
    if final:
        operands += list(finish)
        specs += [smem, vmem, vmem]
    entries = 4
    return pl.pallas_call(
        functools.partial(step_kernel, phase, first, final, places),
        out_shape=jax.ShapeDtypeStruct(
            queries.shape, jnp.bfloat16 if final else jnp.float32
        ),
        in_specs=specs,
        out_specs=vmem if final else hbm,
        scratch_shapes=[
            pltpu.VMEM((depth, length, features), jnp.bfloat16),
            pltpu.VMEM((length, 2 * features), jnp.bfloat16),
            pltpu.VMEM((views, length, features), jnp.float32),
            pltpu.SemaphoreType.DMA((len(arrays) + 1,)),
        ],
        compiler_params=pltpu.CompilerParams(vmem_limit_bytes=56 * 1024 * 1024),
        cost_estimate=pl.CostEstimate(
            flops=entries * length * features * (4 * features + 4 * 4 * length),
            bytes_accessed=8 * views * length * features,
            transcendentals=entries * HEADS * length * length,
        ),
        name="attend_phase",
    )(*operands)


def per_device(tokens, w_query, w_key, w_value, w_out, partners, counts, key_slot):
    views_here, length, features = tokens.shape
    members = lax.axis_size("member")
    groups = lax.axis_size("group")
    me = lax.axis_index("member")
    degree = partners.shape[1]
    slot_key = key_slot[0]
    entry_list = partners.reshape(-1)
    entry_count = entry_list.shape[0]
    capacity = (entry_count + members - 2) // (members - 1)
    peers = entry_list // views_here % members
    places = entry_list % views_here
    order = jnp.arange(entry_count, dtype=jnp.int32)
    same_peer = (peers[:, None] == peers[None, :]) & (order[None, :] < order[:, None])
    ranks = jnp.sum(same_peer.astype(jnp.int32), axis=1)
    live = (jnp.arange(degree, dtype=jnp.int32)[None, :] < counts[:, None]).reshape(-1)
    entry_views = order // degree
    gather = members * views_here <= 2 * entry_count and members % ROW == 0

    own_key = lax.dynamic_slice_in_dim(tokens, slot_key, 1, 0)
    below = lax.ppermute(own_key, "group", [(g, (g + 1) % groups) for g in range(groups)])
    above = lax.ppermute(own_key, "group", [((g + 1) % groups, g) for g in range(groups)])

    normed = layer_norm(tokens).astype(jnp.bfloat16)
    queries = (
        jnp.dot(
            normed.reshape(views_here * length, features),
            w_query,
            preferred_element_type=jnp.float32,
        )
        .astype(jnp.bfloat16)
        .reshape(views_here, length, features)
    )
    w_pair = jnp.concatenate((w_key, w_value), axis=1)
    is_key = (jnp.arange(views_here, dtype=jnp.int32) == slot_key).astype(jnp.int32)
    inverse = 1.0 / (counts + 2 * is_key).astype(jnp.float32)
    finish = (inverse, tokens, w_out)

    def make_table(phases, spots, key_phase, key_spot):
        key_rows = jnp.array([key_spot, key_spot + 1], jnp.int32)
        return jnp.stack(
            (
                jnp.concatenate((jnp.where(live, phases, 0), jnp.full((2,), key_phase, jnp.int32))),
                jnp.concatenate((spots, key_rows)),
                jnp.concatenate((entry_views, jnp.full((2,), 1, jnp.int32) * slot_key)),
            )
        )

    if not gather:
        cells = peers * capacity + ranks
        requests = (
            jnp.zeros((members * capacity,), jnp.int32)
            .at[cells]
            .set(places)
            .reshape(members, capacity)
        )
        asked = lax.all_to_all(requests, "member", split_axis=0, concat_axis=0, tiled=True)
        outgoing = tokens[asked.reshape(-1)].reshape(members, capacity, length, features)
        arrived = lax.all_to_all(outgoing, "member", split_axis=0, concat_axis=0, tiled=True)
        arrived = arrived.reshape(members * capacity, length, features)
        table = make_table(jnp.ones_like(cells), cells, 1, members * capacity)
        blocks = [
            (0, arrived),
            (members * capacity, below),
            (members * capacity + 1, above),
        ]
        return add_phase(1, table, queries, w_pair, blocks, None, finish)

    rows = members // ROW
    my_row, my_side = me // ROW, me % ROW
    peer_rows, peer_sides = peers // ROW, peers % ROW
    across = [(m, m ^ 1) for m in range(members)]

    def shift(block, step, up):
        route = []
        for m in range(members):
            row = m // ROW
            if up and row >= step - 1 and row + 1 < rows:
                route.append((m, m + ROW))
            if not up and row <= rows - step and row >= 1:
                route.append((m, m - ROW))
        return lax.ppermute(block, "member", route)

    def swap(block, step, up):
        route = [
            (m, other)
            for m, other in across
            if (m // ROW >= step if up else m // ROW <= rows - 1 - step)
        ]
        return lax.ppermute(block, "member", route)

    wanted = (
        (peer_rows[None, None, :] == jnp.arange(rows)[:, None, None])
        & (ranks[None, None, :] == jnp.arange(capacity)[None, :, None])
        & (peer_sides != my_side)[None, None, :]
    )
    request = jnp.sum(jnp.where(wanted, places[None, None, :], 0), axis=2)
    asked = lax.ppermute(request, "member", across)

    distance = jnp.abs(peer_rows - my_row)
    beside = peer_sides != my_side
    is_down = (peer_rows > my_row).astype(jnp.int32)
    phases = distance + beside.astype(jnp.int32)
    spots = jnp.where(
        beside,
        2 * views_here + jnp.where(distance == 0, places, is_down * capacity + ranks),
        is_down * views_here + places,
    )
    table = make_table(phases, spots, 1, 3 * views_here)

    ups, downs = [tokens], [tokens]
    side_blocks = [lax.ppermute(tokens, "member", across)]
    for step in range(1, rows):
        ups.append(shift(ups[-1], step, True))
        downs.append(shift(downs[-1], step, False))
    total = None
    for phase in range(1, rows + 1):
        blocks = []
        if phase < rows:
            blocks += [(0, ups[phase]), (views_here, downs[phase])]
        if phase == 1:
            blocks += [
                (2 * views_here, side_blocks[0]),
                (3 * views_here, below),
                (3 * views_here + 1, above),
            ]
        else:
            step = phase - 1
            asked_up = lax.dynamic_index_in_dim(
                asked, jnp.maximum(my_row - step, 0), 0, keepdims=False
            )
            asked_down = lax.dynamic_index_in_dim(
                asked, jnp.minimum(my_row + step, rows - 1), 0, keepdims=False
            )
            blocks += [
                (2 * views_here, swap(ups[step][asked_up], step, True)),
                (2 * views_here + capacity, swap(downs[step][asked_down], step, False)),
            ]
        total = add_phase(
            phase, table, queries, w_pair, blocks, total, finish if phase == rows else None
        )
    return total


def solution(mesh):
    return jax.shard_map(
        per_device,
        mesh=mesh,
        in_specs=(
            P(("group", "member"), None, None),
            P(),
            P(),
            P(),
            P(),
            P(("group", "member"), None),
            P(("group", "member")),
            P(("group", "member")),
        ),
        out_specs=P(("group", "member"), None, None),
        check_vma=False,
    )
```

```python
import functools

import jax
import jax.numpy as jnp
from jax import lax
from jax.experimental import pallas as pl
from jax.experimental.pallas import tpu as pltpu
from jax.experimental.layout import Layout, with_layout_constraint
from jax.sharding import PartitionSpec as P


HEADS = 12
ROW = 2


def layer_norm(values_in):
    values_in = values_in.astype(jnp.float32)
    centre = jnp.mean(values_in, axis=-1, keepdims=True)
    spread = jnp.mean((values_in - centre) ** 2, axis=-1, keepdims=True)
    return (values_in - centre) * lax.rsqrt(spread + 1e-05)


def step_kernel(phase, first, final, places, *refs):
    table, queries, w_key, w_value = refs[:4]
    blocks = refs[4 : 4 + len(places)]
    rest = list(refs[4 + len(places) :])
    if not first:
        total_in = rest.pop(0)
    if final:
        inverse, tokens, w_out = rest[:3]
        rest = rest[3:]
    out_ref = rest.pop(0)
    held, pair, total, sems = rest
    copies = [
        pltpu.make_async_copy(block, held.at[pl.ds(place, block.shape[0])], sems.at[i])
        for i, (place, block) in enumerate(zip(places, blocks))
    ]
    if not first:
        copies.append(pltpu.make_async_copy(total_in, total, sems.at[len(copies)]))
    for copy in copies:
        copy.start()
    if first:
        total[...] = jnp.zeros_like(total)
    for copy in copies:
        copy.wait()
    views, _, features = queries.shape
    size = features // HEADS
    lanes = lax.broadcasted_iota(jnp.int32, (1, 2 * size), 1)
    lower = lanes < size

    def entry(e, carry):
        @pl.when(table[0, e] == phase)
        def _():
            place, view = table[1, e], table[2, e]
            normed = layer_norm(held[place]).astype(jnp.bfloat16)
            pair[:, :features] = jnp.dot(
                normed, w_key[...], preferred_element_type=jnp.float32
            ).astype(jnp.bfloat16)
            pair[:, features:] = jnp.dot(
                normed, w_value[...], preferred_element_type=jnp.float32
            ).astype(jnp.bfloat16)
            for h in range(HEADS // 2):
                cols = pl.ds(2 * h * size, 2 * size)
                query = queries[view, :, cols] * jnp.bfloat16(size**-0.5)
                key = pair[:, cols]
                value = pair[:, pl.ds(features + 2 * h * size, 2 * size)]
                halves = []
                for keep in (lower, jnp.logical_not(lower)):
                    part = jnp.where(keep, query, jnp.zeros_like(query))
                    scores = lax.dot_general(
                        part, key, (((1,), (1,)), ((), ())), preferred_element_type=jnp.float32
                    )
                    top = jnp.max(scores, axis=-1, keepdims=True)
                    weights = jnp.exp(scores - top)
                    mass = jnp.sum(weights, axis=-1, keepdims=True)
                    result = jnp.dot(
                        weights.astype(jnp.bfloat16), value, preferred_element_type=jnp.float32
                    )
                    halves.append(result / mass)
                total[view, :, cols] += jnp.where(lower, halves[0], halves[1])

        return carry

    lax.fori_loop(0, table.shape[1], entry, 0)
    if final:
        for v in range(views):
            mixed = (total[v] * inverse[v]).astype(jnp.bfloat16)
            projected = jnp.dot(mixed, w_out[...], preferred_element_type=jnp.float32)
            out_ref[v] = (tokens[v].astype(jnp.float32) + projected).astype(out_ref.dtype)
    else:
        copy = pltpu.make_async_copy(total, out_ref, sems.at[0])
        copy.start()
        copy.wait()


def add_phase(phase, table, queries, w_key, w_value, blocks, total, finish=None):
    views, length, features = queries.shape
    first, final = total is None, finish is not None
    places = [place for place, _ in blocks]
    arrays = [block for _, block in blocks]
    depth = max(place + block.shape[0] for place, block in blocks)
    vmem = pl.BlockSpec(memory_space=pltpu.VMEM)
    smem = pl.BlockSpec(memory_space=pltpu.SMEM)
    hbm = pl.BlockSpec(memory_space=pl.ANY)
    operands = [table, queries, w_key, w_value, *arrays]
    specs = [smem, vmem, vmem, vmem] + [hbm] * len(arrays)
    if not first:
        operands.append(total)
        specs.append(hbm)
    if final:
        operands += list(finish)
        specs += [smem, vmem, vmem]
    entries = 4
    return pl.pallas_call(
        functools.partial(step_kernel, phase, first, final, places),
        out_shape=jax.ShapeDtypeStruct(
            queries.shape, jnp.bfloat16 if final else jnp.float32
        ),
        in_specs=specs,
        out_specs=vmem if final else hbm,
        scratch_shapes=[
            pltpu.VMEM((depth, length, features), jnp.bfloat16),
            pltpu.VMEM((length, 2 * features), jnp.bfloat16),
            pltpu.VMEM((views, length, features), jnp.float32),
            pltpu.SemaphoreType.DMA((len(arrays) + 1,)),
        ],
        compiler_params=pltpu.CompilerParams(vmem_limit_bytes=56 * 1024 * 1024),
        cost_estimate=pl.CostEstimate(
            flops=entries * length * features * (4 * features + 4 * 4 * length),
            bytes_accessed=8 * views * length * features,
            transcendentals=entries * HEADS * length * length,
        ),
        name="attend_phase",
    )(*operands)


def pick(block, indices):
    def copy_view(index_ref, source, target):
        target[...] = source[...]

    shape = (1,) + block.shape[1:]
    return pl.pallas_call(
        copy_view,
        grid_spec=pltpu.PrefetchScalarGridSpec(
            num_scalar_prefetch=1,
            grid=indices.shape,
            in_specs=[pl.BlockSpec(shape, lambda i, index: (index[i], 0, 0))],
            out_specs=pl.BlockSpec(shape, lambda i, index: (i, 0, 0)),
        ),
        out_shape=jax.ShapeDtypeStruct(indices.shape + block.shape[1:], block.dtype),
        name="pick_views",
    )(indices, block)


def sublayer(tokens, w_query, w_key, w_value, w_out, partners, counts, key_slot):
    views_here, length, features = tokens.shape
    tokens = with_layout_constraint(tokens, Layout(major_to_minor=(0, 1, 2)))
    members = lax.axis_size("member")
    groups = lax.axis_size("group")
    me = lax.axis_index("member")
    degree = partners.shape[1]
    slot_key = key_slot[0]
    entry_list = partners.reshape(-1)
    entry_count = entry_list.shape[0]
    capacity = (entry_count + members - 2) // (members - 1)
    peers = entry_list // views_here % members
    places = entry_list % views_here
    order = jnp.arange(entry_count, dtype=jnp.int32)
    same_peer = (peers[:, None] == peers[None, :]) & (order[None, :] < order[:, None])
    ranks = jnp.sum(same_peer.astype(jnp.int32), axis=1)
    live = (jnp.arange(degree, dtype=jnp.int32)[None, :] < counts[:, None]).reshape(-1)
    entry_views = order // degree
    gather = members * views_here <= 2 * entry_count and members % ROW == 0

    def keyframes(after=None):
        slot = slot_key if after is None else lax.optimization_barrier((slot_key, after))[0]
        own_key = lax.dynamic_slice_in_dim(tokens, slot, 1, 0)
        below = lax.ppermute(own_key, "group", [(g, (g + 1) % groups) for g in range(groups)])
        above = lax.ppermute(own_key, "group", [((g + 1) % groups, g) for g in range(groups)])
        return below, above

    normed = layer_norm(tokens).astype(jnp.bfloat16)
    queries = (
        jnp.dot(
            normed.reshape(views_here * length, features),
            w_query,
            preferred_element_type=jnp.float32,
        )
        .astype(jnp.bfloat16)
        .reshape(views_here, length, features)
    )
    is_key = (jnp.arange(views_here, dtype=jnp.int32) == slot_key).astype(jnp.int32)
    inverse = 1.0 / (counts + 2 * is_key).astype(jnp.float32)
    finish = (inverse, tokens, w_out)

    def make_table(phases, spots, key_phase, key_spot):
        key_rows = jnp.array([key_spot, key_spot + 1], jnp.int32)
        return jnp.stack(
            (
                jnp.concatenate((jnp.where(live, phases, 0), jnp.full((2,), key_phase, jnp.int32))),
                jnp.concatenate((spots, key_rows)),
                jnp.concatenate((entry_views, jnp.full((2,), 1, jnp.int32) * slot_key)),
            )
        )

    if not gather:
        cells = peers * capacity + ranks
        requests = (
            jnp.zeros((members * capacity,), jnp.int32)
            .at[cells]
            .set(places)
            .reshape(members, capacity)
        )
        asked = lax.all_to_all(requests, "member", split_axis=0, concat_axis=0, tiled=True)
        outgoing = tokens[asked.reshape(-1)].reshape(members, capacity, length, features)
        arrived = lax.all_to_all(outgoing, "member", split_axis=0, concat_axis=0, tiled=True)
        arrived = arrived.reshape(members * capacity, length, features)
        table = make_table(jnp.ones_like(cells), cells, 1, members * capacity)
        below, above = keyframes()
        blocks = [
            (0, arrived),
            (members * capacity, below),
            (members * capacity + 1, above),
        ]
        return add_phase(1, table, queries, w_key, w_value, blocks, None, finish)

    rows = members // ROW
    my_row, my_side = me // ROW, me % ROW
    peer_rows, peer_sides = peers // ROW, peers % ROW
    across = [(m, m ^ 1) for m in range(members)]

    def shift(block, step, up):
        route = []
        for m in range(members):
            row = m // ROW
            if up and row >= step - 1 and row + 1 < rows:
                route.append((m, m + ROW))
            if not up and row <= rows - step and row >= 1:
                route.append((m, m - ROW))
        return lax.ppermute(block, "member", route)

    def swap(block, step, up):
        route = [
            (m, other)
            for m, other in across
            if (m // ROW >= step if up else m // ROW <= rows - 1 - step)
        ]
        return lax.ppermute(block, "member", route)

    wanted = (
        (peer_rows[None, None, :] == jnp.arange(rows)[:, None, None])
        & (ranks[None, None, :] == jnp.arange(capacity)[None, :, None])
        & (peer_sides != my_side)[None, None, :]
    )
    request = jnp.sum(jnp.where(wanted, places[None, None, :], 0), axis=2)
    asked = lax.ppermute(request, "member", across)

    distance = jnp.abs(peer_rows - my_row)
    beside = peer_sides != my_side
    is_down = (peer_rows > my_row).astype(jnp.int32)
    phases = distance + beside.astype(jnp.int32)
    spots = jnp.where(
        beside,
        2 * views_here + jnp.where(distance == 0, places, is_down * capacity + ranks),
        is_down * views_here + places,
    )
    below, above = keyframes(asked)
    key_spot = 2 * views_here + 2 * capacity
    table = make_table(phases, spots, 2, key_spot)

    ups, downs = [tokens], [tokens]
    side_block = lax.ppermute(tokens, "member", across)
    for step in range(1, rows):
        ups.append(shift(ups[-1], step, True))
        downs.append(shift(downs[-1], step, False))
    total = None
    for phase in range(1, rows + 1):
        blocks = []
        if phase < rows:
            blocks += [(0, ups[phase]), (views_here, downs[phase])]
        if phase == 1:
            blocks.append((2 * views_here, side_block))
        else:
            step = phase - 1
            asked_up = lax.dynamic_index_in_dim(
                asked, jnp.maximum(my_row - step, 0), 0, keepdims=False
            )
            asked_down = lax.dynamic_index_in_dim(
                asked, jnp.minimum(my_row + step, rows - 1), 0, keepdims=False
            )
            blocks += [
                (2 * views_here, swap(pick(ups[step], asked_up), step, True)),
                (2 * views_here + capacity, swap(pick(downs[step], asked_down), step, False)),
            ]
        if phase == 2:
            blocks += [(key_spot, below), (key_spot + 1, above)]
        total = add_phase(
            phase,
            table,
            queries,
            w_key,
            w_value,
            blocks,
            total,
            finish if phase == rows else None,
        )
    return total


def solution(mesh):
    return jax.shard_map(
        sublayer,
        mesh=mesh,
        in_specs=(
            P(("group", "member"), None, None),
            P(),
            P(),
            P(),
            P(),
            P(("group", "member"), None),
            P(("group", "member")),
            P(("group", "member")),
        ),
        out_specs=P(("group", "member"), None, None),
        check_vma=False,
    )
```

```python
import functools

import jax
import jax.numpy as jnp
from jax import lax
from jax.experimental import pallas as pl
from jax.experimental.pallas import tpu as pltpu
from jax.sharding import PartitionSpec as P


HEADS = 12
ROW = 2


def layer_norm(values_in):
    values_in = values_in.astype(jnp.float32)
    centre = jnp.mean(values_in, axis=-1, keepdims=True)
    spread = jnp.mean((values_in - centre) ** 2, axis=-1, keepdims=True)
    return (values_in - centre) * lax.rsqrt(spread + 1e-05)


def step_kernel(phase, first, final, places, *refs):
    table, queries, w_key, w_value = refs[:4]
    blocks = refs[4 : 4 + len(places)]
    rest = list(refs[4 + len(places) :])
    if not first:
        total_in = rest.pop(0)
    if final:
        inverse, tokens, w_out = rest[:3]
        rest = rest[3:]
    out_ref = rest.pop(0)
    held, pair, total, sems = rest
    copies = [
        pltpu.make_async_copy(block, held.at[pl.ds(place, block.shape[0])], sems.at[i])
        for i, (place, block) in enumerate(zip(places, blocks))
    ]
    if not first:
        copies.append(pltpu.make_async_copy(total_in, total, sems.at[len(copies)]))
    for copy in copies:
        copy.start()
    if first:
        total[...] = jnp.zeros_like(total)
    for copy in copies:
        copy.wait()
    views, length, features = total.shape
    size = features // HEADS
    lanes = lax.broadcasted_iota(jnp.int32, (1, 2 * size), 1)
    lower = lanes < size

    def entry(e, carry):
        @pl.when(table[0, e] == phase)
        def _():
            place, view = table[1, e], table[2, e]
            normed = layer_norm(held[place, :length, :]).astype(jnp.bfloat16)
            pair[:, :features] = jnp.dot(
                normed, w_key[...], preferred_element_type=jnp.float32
            ).astype(jnp.bfloat16)
            pair[:, features:] = jnp.dot(
                normed, w_value[...], preferred_element_type=jnp.float32
            ).astype(jnp.bfloat16)
            for h in range(HEADS // 2):
                cols = pl.ds(2 * h * size, 2 * size)
                query = queries[view, :length, cols] * jnp.bfloat16(size**-0.5)
                key = pair[:, cols]
                value = pair[:, pl.ds(features + 2 * h * size, 2 * size)]
                halves = []
                for keep in (lower, jnp.logical_not(lower)):
                    part = jnp.where(keep, query, jnp.zeros_like(query))
                    scores = lax.dot_general(
                        part, key, (((1,), (1,)), ((), ())), preferred_element_type=jnp.float32
                    )
                    top = jnp.max(scores, axis=-1, keepdims=True)
                    weights = jnp.exp(scores - top)
                    mass = jnp.sum(weights, axis=-1, keepdims=True)
                    result = jnp.dot(
                        weights.astype(jnp.bfloat16), value, preferred_element_type=jnp.float32
                    )
                    halves.append(result / mass)
                total[view, :, cols] += jnp.where(lower, halves[0], halves[1])

        return carry

    lax.fori_loop(0, table.shape[1], entry, 0)
    if final:
        for v in range(views):
            mixed = (total[v] * inverse[v]).astype(jnp.bfloat16)
            projected = jnp.dot(mixed, w_out[...], preferred_element_type=jnp.float32)
            out_ref[v] = (tokens[v, :length, :].astype(jnp.float32) + projected).astype(out_ref.dtype)
    else:
        copy = pltpu.make_async_copy(total, out_ref, sems.at[0])
        copy.start()
        copy.wait()


def add_phase(length, phase, table, queries, w_key, w_value, blocks, total, finish=None):
    views, padded, features = queries.shape
    first, final = total is None, finish is not None
    places = [place for place, _ in blocks]
    arrays = [block for _, block in blocks]
    depth = max(place + block.shape[0] for place, block in blocks)
    vmem = pl.BlockSpec(memory_space=pltpu.VMEM)
    smem = pl.BlockSpec(memory_space=pltpu.SMEM)
    hbm = pl.BlockSpec(memory_space=pl.ANY)
    operands = [table, queries, w_key, w_value, *arrays]
    specs = [smem, vmem, vmem, vmem] + [hbm] * len(arrays)
    if not first:
        operands.append(total)
        specs.append(hbm)
    if final:
        operands += list(finish)
        specs += [smem, vmem, vmem]
    entries = 4
    return pl.pallas_call(
        functools.partial(step_kernel, phase, first, final, places),
        out_shape=jax.ShapeDtypeStruct(
            (views, length, features), jnp.bfloat16 if final else jnp.float32
        ),
        in_specs=specs,
        out_specs=vmem if final else hbm,
        scratch_shapes=[
            pltpu.VMEM((depth, padded, features), jnp.bfloat16),
            pltpu.VMEM((length, 2 * features), jnp.bfloat16),
            pltpu.VMEM((views, length, features), jnp.float32),
            pltpu.SemaphoreType.DMA((len(arrays) + 1,)),
        ],
        compiler_params=pltpu.CompilerParams(vmem_limit_bytes=56 * 1024 * 1024),
        cost_estimate=pl.CostEstimate(
            flops=entries * length * features * (4 * features + 4 * 4 * length),
            bytes_accessed=8 * views * length * features,
            transcendentals=entries * HEADS * length * length,
        ),
        name="attend_phase",
    )(*operands)


def pick(block, indices):
    def copy_views(index, source, target, sems):
        copies = [
            pltpu.make_async_copy(source.at[index[i]], target.at[i], sems.at[i])
            for i in range(target.shape[0])
        ]
        for copy in copies:
            copy.start()
        for copy in copies:
            copy.wait()

    return pl.pallas_call(
        copy_views,
        in_specs=[
            pl.BlockSpec(memory_space=pltpu.SMEM),
            pl.BlockSpec(memory_space=pl.ANY),
        ],
        out_specs=pl.BlockSpec(memory_space=pltpu.VMEM),
        out_shape=jax.ShapeDtypeStruct(indices.shape + block.shape[1:], block.dtype),
        scratch_shapes=[pltpu.SemaphoreType.DMA(indices.shape)],
        name="pick_views",
    )(indices, block)


def sublayer(tokens, w_query, w_key, w_value, w_out, partners, counts, key_slot):
    views_here, length, features = tokens.shape
    tokens = jnp.pad(tokens, ((0, 0), (0, -length % 8), (0, 0)))
    padded = tokens.shape[1]
    members = lax.axis_size("member")
    groups = lax.axis_size("group")
    me = lax.axis_index("member")
    degree = partners.shape[1]
    slot_key = key_slot[0]
    entry_list = partners.reshape(-1)
    entry_count = entry_list.shape[0]
    capacity = (entry_count + members - 2) // (members - 1)
    peers = entry_list // views_here % members
    places = entry_list % views_here
    order = jnp.arange(entry_count, dtype=jnp.int32)
    same_peer = (peers[:, None] == peers[None, :]) & (order[None, :] < order[:, None])
    ranks = jnp.sum(same_peer.astype(jnp.int32), axis=1)
    live = (jnp.arange(degree, dtype=jnp.int32)[None, :] < counts[:, None]).reshape(-1)
    entry_views = order // degree
    gather = members * views_here <= 2 * entry_count and members % ROW == 0

    def keyframes(after=None):
        slot = slot_key if after is None else lax.optimization_barrier((slot_key, after))[0]
        own_key = lax.dynamic_slice_in_dim(tokens, slot, 1, 0)
        below = lax.ppermute(own_key, "group", [(g, (g + 1) % groups) for g in range(groups)])
        above = lax.ppermute(own_key, "group", [((g + 1) % groups, g) for g in range(groups)])
        return below, above

    normed = layer_norm(tokens).astype(jnp.bfloat16)
    queries = jnp.dot(
        normed.reshape(views_here * padded, features),
        w_query,
        preferred_element_type=jnp.float32,
    ).astype(jnp.bfloat16)
    queries = queries.reshape(views_here, padded, features)
    is_key = (jnp.arange(views_here, dtype=jnp.int32) == slot_key).astype(jnp.int32)
    inverse = 1.0 / (counts + 2 * is_key).astype(jnp.float32)
    finish = (inverse, tokens, w_out)

    def make_table(phases, spots, key_phase, key_spot):
        key_rows = jnp.array([key_spot, key_spot + 1], jnp.int32)
        return jnp.stack(
            (
                jnp.concatenate((jnp.where(live, phases, 0), jnp.full((2,), key_phase, jnp.int32))),
                jnp.concatenate((spots, key_rows)),
                jnp.concatenate((entry_views, jnp.full((2,), 1, jnp.int32) * slot_key)),
            )
        )

    if not gather:
        cells = peers * capacity + ranks
        requests = (
            jnp.zeros((members * capacity,), jnp.int32)
            .at[cells]
            .set(places)
            .reshape(members, capacity)
        )
        asked = lax.all_to_all(requests, "member", split_axis=0, concat_axis=0, tiled=True)
        outgoing = tokens[asked.reshape(-1)].reshape(members, capacity, padded, features)
        arrived = lax.all_to_all(outgoing, "member", split_axis=0, concat_axis=0, tiled=True)
        arrived = arrived.reshape(members * capacity, padded, features)
        table = make_table(jnp.ones_like(cells), cells, 1, members * capacity)
        below, above = keyframes()
        blocks = [
            (0, arrived),
            (members * capacity, below),
            (members * capacity + 1, above),
        ]
        return add_phase(length, 1, table, queries, w_key, w_value, blocks, None, finish)

    rows = members // ROW
    my_row, my_side = me // ROW, me % ROW
    peer_rows, peer_sides = peers // ROW, peers % ROW
    across = [(m, m ^ 1) for m in range(members)]

    def shift(block, step, up):
        route = []
        for m in range(members):
            row = m // ROW
            if up and row >= step - 1 and row + 1 < rows:
                route.append((m, m + ROW))
            if not up and row <= rows - step and row >= 1:
                route.append((m, m - ROW))
        return lax.ppermute(block, "member", route)

    def swap(block, step, up):
        route = [
            (m, other)
            for m, other in across
            if (m // ROW >= step if up else m // ROW <= rows - 1 - step)
        ]
        return lax.ppermute(block, "member", route)

    wanted = (
        (peer_rows[None, None, :] == jnp.arange(rows)[:, None, None])
        & (ranks[None, None, :] == jnp.arange(capacity)[None, :, None])
        & (peer_sides != my_side)[None, None, :]
    )
    request = jnp.sum(jnp.where(wanted, places[None, None, :], 0), axis=2)
    asked = lax.ppermute(request, "member", across)

    distance = jnp.abs(peer_rows - my_row)
    beside = peer_sides != my_side
    is_down = (peer_rows > my_row).astype(jnp.int32)
    phases = distance + beside.astype(jnp.int32)
    spots = jnp.where(
        beside,
        2 * views_here + jnp.where(distance == 0, places, is_down * capacity + ranks),
        is_down * views_here + places,
    )
    below, above = keyframes(asked)
    key_spot = 2 * views_here + 2 * capacity
    table = make_table(phases, spots, 2, key_spot)

    ups, downs = [tokens], [tokens]
    side_block = lax.ppermute(tokens, "member", across)
    for step in range(1, rows):
        ups.append(shift(ups[-1], step, True))
        downs.append(shift(downs[-1], step, False))
    total = None
    for phase in range(1, rows + 1):
        blocks = []
        if phase < rows:
            blocks += [(0, ups[phase]), (views_here, downs[phase])]
        if phase == 1:
            blocks.append((2 * views_here, side_block))
        else:
            step = phase - 1
            asked_up = lax.dynamic_index_in_dim(
                asked, jnp.maximum(my_row - step, 0), 0, keepdims=False
            )
            asked_down = lax.dynamic_index_in_dim(
                asked, jnp.minimum(my_row + step, rows - 1), 0, keepdims=False
            )
            blocks += [
                (2 * views_here, swap(pick(ups[step], asked_up), step, True)),
                (2 * views_here + capacity, swap(pick(downs[step], asked_down), step, False)),
            ]
        if phase == 2:
            blocks += [(key_spot, below), (key_spot + 1, above)]
        total = add_phase(
            length,
            phase,
            table,
            queries,
            w_key,
            w_value,
            blocks,
            total,
            finish if phase == rows else None,
        )
    return total


def solution(mesh):
    return jax.shard_map(
        sublayer,
        mesh=mesh,
        in_specs=(
            P(("group", "member"), None, None),
            P(),
            P(),
            P(),
            P(),
            P(("group", "member"), None),
            P(("group", "member")),
            P(("group", "member")),
        ),
        out_specs=P(("group", "member"), None, None),
        check_vma=False,
    )
```
